32 devices in a mesh: groups: 1, seq: 32 (over z, y, x, core).
Axes of the slice: x: 2, y: 2, z: 4, core: 2. Of those that a mesh axis runs over, the one named last changes fastest.
Arguments:
- features: bfloat16 [4096, 768], P(('groups', 'seq')), may hold values from -6 to 6
- first_layer_taps: bfloat16 [3, 768, 768], replicated, may hold values from -0.125 to 0.125
- second_layer_taps: bfloat16 [3, 768, 768], replicated, may hold values from -0.125 to 0.125
- upstream: bfloat16 [4096, 768], P(('groups', 'seq')), may hold values from -6 to 6
Outputs:
- second_layer_output: bfloat16 [4096, 768], P(('groups', 'seq'))
- input_gradient: bfloat16 [4096, 768], P(('groups', 'seq'))
- first_taps_gradient: float32 [3, 768, 768], P(None, 'groups', 'seq')
The draws below stay inside these ranges and needn't reach their ends.
All inputs are finite; a program needn't handle non-finite values.
Results may differ from the reference program's by a relative error of at most 0.0095.
Values may be sent and summed in bfloat16 or wider, within the bound.
No kernel may reach another device: no remote copies, remote signals or barrier semaphores. Data moves between devices by JAX's collectives and lax.ppermute only.
A program may use at most 128 MiB of HBM per device.

```python
import jax
import jax.numpy as jnp

C = 768
DILATION_ONE = 256
DILATION_TWO = 2048
BINS = 4096


def strengthened(entries, rng, source, target, shards_of, factor):
    def block_of(dim):
        return (jnp.arange(entries.shape[dim]) // (entries.shape[dim] // shards_of)).reshape((-1,) + (1,) * (entries.ndim - 1 - dim))

    first = jax.random.permutation(rng, shards_of)[block_of(target)]
    far = (block_of(target) + shards_of // 2) % shards_of
    return jnp.where((block_of(source) == first) | (block_of(source) == far), factor * entries, entries)


def block_scale(rng, extent, cuts, low, top_value):
    level, own = 1.0, jax.random.fold_in(rng, 6)
    for dim, shards_of in cuts:
        heights = jnp.exp(jax.random.uniform(jax.random.fold_in(own, dim), (shards_of,), jnp.float32, low / len(cuts), top_value / len(cuts)))
        level = level * jnp.repeat(heights, extent[dim] // shards_of).reshape([-1 if axis == dim else 1 for axis in range(len(extent))])
    return level


def noise(rng, shape, deviation, limit, cuts=(), kind=jnp.bfloat16):
    gain = block_scale(rng, shape, cuts, -0.22, 0.18) if cuts else 1.0
    values = jax.random.normal(rng, shape, jnp.float32) * deviation * gain
    return jnp.minimum(jnp.maximum(values, -limit), limit).astype(kind)


def heavy_noise(rng, extent, width, most, cuts, heavy, held_as=jnp.bfloat16):
    drawn = width * jax.random.normal(rng, extent, jnp.float32)
    if cuts:
        drawn = drawn * block_scale(rng, extent, cuts, -0.22, 0.18)
    return jnp.clip(strengthened(drawn, jax.random.fold_in(rng, 3), *heavy), -most, most).astype(held_as)


def setup_inputs(seed: int = 0, part: int = 0) -> dict:
    seeds = jax.random.split(jax.random.key(seed), 5)
    part_splits = jax.random.split(jax.random.fold_in(seeds[4], part), 5)
    features = noise(part_splits[0], (BINS, C), 1.0, 6.0, ((0, 32),))
    first_layer_taps = noise(seeds[1], (3, C, C), (3 * C) ** -0.5, 0.125)
    second_layer_taps = noise(seeds[2], (3, C, C), (3 * C) ** -0.5, 0.125)
    upstream = heavy_noise(part_splits[3], (BINS, C), 1.0, 6.0, ((0, 32),), (0, 1, 32, 2.75))
    return dict(features=features, first_layer_taps=first_layer_taps, second_layer_taps=second_layer_taps, upstream=upstream)


def gelu_pair(values):
    wide = values.astype(jnp.float32)
    return jax.jvp(jax.nn.gelu, (wide,), (jnp.ones_like(wide),))


def shifted(values, offset):
    pad = jnp.zeros((abs(offset), values.shape[1]), values.dtype)
    if offset > 0:
        return jnp.concatenate([values[offset:], pad], 0)
    return jnp.concatenate([pad, values[:offset]], 0)


def residual_layer_forward(inputs, kernel, dilation):
    acts = gelu_pair(inputs)[0].astype(jnp.bfloat16)
    conv = jnp.zeros(inputs.shape, jnp.float32)
    for k in range(3):
        offset = (k - 1) * dilation
        source = acts if offset == 0 else shifted(acts, offset)
        conv = conv + jnp.dot(source, kernel[k], preferred_element_type=jnp.float32)
    outputs = (inputs.astype(jnp.float32) + conv).astype(jnp.bfloat16)
    return acts, outputs


def residual_layer_backward(inputs, acts, kernel, cotan, dilation, want_grads):
    back = jnp.zeros(inputs.shape, jnp.float32)
    grads = []
    for k in range(3):
        offset = -(k - 1) * dilation
        moved = cotan if offset == 0 else shifted(cotan, offset)
        back = back + jnp.dot(moved, kernel[k].T, preferred_element_type=jnp.float32)
        if want_grads:
            grads.append(jnp.dot(acts.T, moved, preferred_element_type=jnp.float32))
    slope = gelu_pair(inputs)[1]
    result = (cotan.astype(jnp.float32) + slope * back).astype(jnp.bfloat16)
    if want_grads:
        return result, jnp.stack(grads, 0)
    return result, None


def reference(features, first_layer_taps, second_layer_taps, upstream):
    first_layer_activations, first_layer_output = residual_layer_forward(features, first_layer_taps, DILATION_ONE)
    second_layer_activations, second_layer_output = residual_layer_forward(first_layer_output, second_layer_taps, DILATION_TWO)
    middle_gradient, unused_terms = residual_layer_backward(first_layer_output, second_layer_activations, second_layer_taps, upstream, DILATION_TWO, False)
    input_gradient, first_taps_gradient = residual_layer_backward(features, first_layer_activations, first_layer_taps, middle_gradient, DILATION_ONE, True)
    return second_layer_output, input_gradient, first_taps_gradient
```

```python
import jax
import jax.numpy as jnp
from jax import lax
from jax.sharding import PartitionSpec as P

DILATION_ONE = 256
DILATION_TWO = 2048
PLANE = 8


def moved(array, target):
    size = lax.axis_size("seq")
    pairs = [(i, target(i)) for i in range(size)]
    pairs = [(i, t) for i, t in pairs if t is not None and 0 <= t < size]
    return lax.ppermute(array, "seq", pairs)


def gelu_pair(values):
    wide = values.astype(jnp.float32)
    return jax.jvp(jax.nn.gelu, (wide,), (jnp.ones_like(wide),))


def dot(a, b):
    return jnp.dot(a, b, preferred_element_type=jnp.float32)


def dot_t(a, b):
    return jnp.einsum("bo,io->bi", a, b, preferred_element_type=jnp.float32)


def far_terms(values, taps, sign, product):
    size = lax.axis_size("seq")
    steps = DILATION_TWO // values.shape[0]
    if 2 * steps == size:
        other = moved(values, lambda i: i ^ steps)
        first = lax.axis_index("seq") < steps
        tap = jnp.where(first, 1 + sign, 1 - sign)
        return product(other, lax.dynamic_index_in_dim(taps, tap, 0, keepdims=False))
    behind = moved(values, lambda i: i + steps)
    ahead = moved(values, lambda i: i - steps)
    return product(behind, taps[1 - sign]) + product(ahead, taps[1 + sign])


def pick(stack, at):
    return lax.dynamic_index_in_dim(stack, at, 0, keepdims=False)


def local(features, first_taps, second_taps, upstream):
    size = lax.axis_size("seq")
    planes = size // PLANE
    rows, width = features.shape
    own_cols = width // size
    index = lax.axis_index("seq")
    plane, chip, core = index // PLANE, (index // 2) % 4, index % 2

    acts, slope_first = gelu_pair(features)
    acts = acts.astype(jnp.bfloat16)
    far_up = far_terms(upstream, second_taps, -1, dot_t)

    near = [acts] + [moved(acts, lambda i, s=s: i ^ (2 * s)) for s in (1, 3, 2)]
    near = jnp.stack([near[0], near[1], near[3], near[2]])
    edge = moved(acts, lambda i: {0: i - 2, 3: i + 2}.get((i // 2) % 4))
    acts_back = jnp.where(chip == 0, edge, pick(near, (chip - 1) % 4 ^ chip))
    acts_ahead = jnp.where(chip == 3, edge, pick(near, (chip + 1) % 4 ^ chip))

    conv = dot(acts, first_taps[1]) + dot(acts_back, first_taps[0]) + dot(acts_ahead, first_taps[2])
    output_first = (features.astype(jnp.float32) + conv).astype(jnp.bfloat16)
    acts_second, slope_second = gelu_pair(output_first)
    acts_second = acts_second.astype(jnp.bfloat16)

    back = dot_t(upstream, second_taps[1]) + far_up
    middle = (upstream.astype(jnp.float32) + slope_second * back).astype(jnp.bfloat16)

    turned = middle.T.reshape(planes, 4, 2, own_cols, rows).transpose(1, 2, 0, 3, 4)
    parts = [pick(turned, chip ^ s) for s in range(4)]
    parts = [parts[0]] + [moved(parts[s], lambda i, s=s: i ^ (2 * s)) for s in (1, 2, 3)]
    parts = jnp.stack(parts)
    other_cols = moved(lax.dynamic_index_in_dim(parts, 1 - core, 1, keepdims=False), lambda i: i ^ 1)
    own_parts = lax.dynamic_index_in_dim(parts, core, 1, keepdims=False)

    ordered = [pick(near, s ^ chip) for s in range(4)]
    halo_back = moved(ordered[3], lambda i: i + PLANE)
    halo_ahead = moved(ordered[0], lambda i: i - PLANE)
    line = jnp.concatenate([halo_back] + ordered + [halo_ahead])
    other_line = moved(line, lambda i: i ^ 1)

    def side(cols):
        ordered_cols = [pick(cols, s ^ chip).reshape(-1, rows) for s in range(4)]
        return jnp.concatenate(ordered_cols, 1)

    own_side, other_side = side(own_parts), side(other_cols)
    terms = []
    for k in range(3):
        span = slice(k * rows, (k + 4) * rows)
        terms.append(dot(own_side, line[span]) + dot(other_side, other_line[span]))
    terms = jnp.stack(terms).reshape(3, planes, own_cols, width)

    if planes == 4:
        total = lax.dynamic_index_in_dim(terms, plane, 1, keepdims=False)
        for s in (3, 2, 1):
            piece = lax.dynamic_index_in_dim(terms, plane ^ s, 1, keepdims=False)
            got = moved(piece.astype(jnp.bfloat16), lambda i, s=s: i ^ (PLANE * s))
            total = total + got.astype(jnp.float32)
    else:
        lines = [list(range(r, size, PLANE)) for r in range(PLANE)]
        total = lax.psum_scatter(terms, "seq", scatter_dimension=1, axis_index_groups=lines)
    first_taps_gradient = jnp.swapaxes(total, 1, 2)

    conv_second = dot(acts_second, second_taps[1]) + far_terms(acts_second, second_taps, 1, dot)
    second_layer_output = (output_first.astype(jnp.float32) + conv_second).astype(jnp.bfloat16)

    behind = moved(middle, lambda i: i + 2)
    ahead = moved(middle, lambda i: i - 2)
    back_first = (
        dot_t(middle, first_taps[1]) + dot_t(ahead, first_taps[0]) + dot_t(behind, first_taps[2])
    )
    input_gradient = (middle.astype(jnp.float32) + slope_first * back_first).astype(jnp.bfloat16)
    return second_layer_output, input_gradient, first_taps_gradient


def solution(mesh):
    placed = (P(("groups", "seq"), None), P(), P(), P(("groups", "seq"), None))
    return jax.shard_map(
        local,
        mesh=mesh,
        in_specs=placed,
        out_specs=(
            P(("groups", "seq"), None),
            P(("groups", "seq"), None),
            P(None, "groups", "seq"),
        ),
        check_vma=False,
    )
```

```python
import functools

import jax
import jax.numpy as jnp
from jax import lax
from jax.experimental import pallas as pl
from jax.experimental.pallas import tpu as pltpu
from jax.sharding import PartitionSpec as P

DILATION_ONE = 256
DILATION_TWO = 2048
PLANE = 8
LIMIT = 8 * 2**20
F32 = jnp.float32
BF16 = jnp.bfloat16


def moved(array, target):
    size = lax.axis_size("seq")
    pairs = [(i, target(i)) for i in range(size)]
    pairs = [(i, t) for i, t in pairs if t is not None and 0 <= t < size]
    return lax.ppermute(array, "seq", pairs)


def after(value, *first):
    return lax.optimization_barrier((value, *first))[0]


def gelu_pair(values):
    wide = values.astype(F32)
    return jax.jvp(jax.nn.gelu, (wide,), (jnp.ones_like(wide),))


def dot(a, b):
    return jnp.dot(a, b, preferred_element_type=F32)


def dot_t(a, b):
    return lax.dot_general(a, b, (((1,), (1,)), ((), ())), preferred_element_type=F32)


def call(body, name, outs, *arrays, scratch=()):
    vmem = pl.BlockSpec(memory_space=pltpu.VMEM)
    return pl.pallas_call(
        body,
        name=name,
        out_shape=[jax.ShapeDtypeStruct(shape, kind) for shape, kind in outs],
        in_specs=[vmem] * len(arrays),
        out_specs=[vmem] * len(outs),
        scratch_shapes=list(scratch),
        compiler_params=pltpu.CompilerParams(vmem_limit_bytes=LIMIT),
    )(*arrays)


def position(rows):
    index = lax.axis_index("seq")
    lower = (index < DILATION_TWO // rows).astype(jnp.int32)
    return (index >> 1) & 3, index & 1, index >> 3, lower


def center_body(features, acts, up, taps, second_taps, conv, back, slope):
    conv[...] = features[...].astype(F32) + dot(acts[...], taps[1])
    back[...] = dot_t(up[...], second_taps[1])
    slope[...] = gelu_pair(features[...])[1]


def line_body(acts, flip, turn, cross, line, line_first, line_last):
    rows = acts.shape[0]
    chip = position(rows)[0]
    for slot, piece in enumerate((acts, flip, cross, turn)):
        value = piece[...]
        line[pl.ds((chip ^ slot) * rows, rows)] = value

        @pl.when(chip == slot)
        def _():
            line_first[...] = value

        @pl.when(chip == (slot ^ 3))
        def _():
            line_last[...] = value


def middle_body(far, *refs, planes):
    *others, line, edge, conv, up, back, taps, second_taps = refs[:-9]
    output, acts_second, middle, own, one, two, three, turned, near = refs[-9:]
    rows = edge.shape[0]
    chip, own_core, _, first = position(rows)
    near[0] = line[pl.ds(jnp.maximum(chip - 1, 0) * rows, rows)]
    near[1] = line[pl.ds(jnp.minimum(chip + 1, 3) * rows, rows)]

    @pl.when(chip == 0)
    def _():
        near[0] = edge[...]

    @pl.when(chip == 3)
    def _():
        near[1] = edge[...]

    result = (conv[...] + dot(near[0], taps[0]) + dot(near[1], taps[2])).astype(BF16)
    output[...] = result
    activated, slope = gelu_pair(result)
    acts_second[...] = activated.astype(BF16)
    total = back[...]
    if others:
        total = total + dot_t(others[0][...], second_taps[0]) + dot_t(far[...], second_taps[2])
    else:
        total = total + dot_t(far[...], second_taps[2 - 2 * first])
    value = (up[...].astype(F32) + slope * total).astype(BF16)
    middle[...] = value
    flat = value.astype(F32).T
    own_cols = turned.shape[1] // planes
    for z in range(planes):
        for owner in range(PLANE):
            start = (z * PLANE + owner) * own_cols
            turned[owner, z * own_cols : (z + 1) * own_cols] = flat[start : start + own_cols]
    for slot, out in enumerate((own, one, two, three)):
        for other in range(2):
            out[other] = turned[2 * (chip ^ slot) + (own_core ^ other)].astype(BF16)


def terms_body(*refs, planes):
    parts = refs[0:4]
    other_parts, line, other_line = refs[4:7]
    halo_back, halo_ahead, other_back, other_ahead = refs[7:11]
    outs, (cols, whole, sums) = refs[11:-3], refs[-3:]
    rows = halo_back.shape[0]
    chip, _, plane, _ = position(rows)
    for b in range(4):
        slot = b ^ chip
        for s in range(4):

            @pl.when(slot == s)
            def _():
                cols[0, :, b * rows : (b + 1) * rows] = parts[s][0]
                cols[1, :, b * rows : (b + 1) * rows] = other_parts[s]

    for side, pieces in enumerate(((halo_back, line, halo_ahead), (other_back, other_line, other_ahead))):
        whole[side, :rows] = pieces[0][...]
        whole[side, rows : 5 * rows] = pieces[1][...]
        whole[side, 5 * rows :] = pieces[2][...]
    own_cols = sums.shape[2]
    for k in range(3):
        span = slice(k * rows, (k + 4) * rows)
        value = dot(cols[0], whole[0, span]) + dot(cols[1], whole[1, span])
        for z in range(planes):
            sums[k, z] = value[z * own_cols : (z + 1) * own_cols]
    if len(outs) == 1:
        outs[0][...] = sums[...]
    else:
        for k in range(3):
            outs[0][k] = sums[k, plane]
            for s in range(1, 4):
                outs[s][k] = sums[k, plane ^ s].astype(BF16)


def second_forward(far, *refs):
    *others, acts, output_first, taps, output = refs
    first = position(acts.shape[0])[3]
    conv = dot(acts[...], taps[1])
    if others:
        conv = conv + dot(others[0][...], taps[2]) + dot(far[...], taps[0])
    else:
        conv = conv + dot(far[...], taps[2 * first])
    output[...] = (output_first[...].astype(F32) + conv).astype(BF16)


def first_backward(middle, behind, ahead, slope, taps, output):
    back = dot_t(middle[...], taps[1]) + dot_t(ahead[...], taps[0]) + dot_t(behind[...], taps[2])
    output[...] = (middle[...].astype(F32) + slope[...] * back).astype(BF16)


def far_pieces(values):
    size = lax.axis_size("seq")
    steps = DILATION_TWO // values.shape[0]
    if 2 * steps == size:
        return [moved(values, lambda i: i ^ steps)]
    return [moved(values, lambda i: i + steps), moved(values, lambda i: i - steps)]


def local(features, first_taps, second_taps, upstream):
    size = lax.axis_size("seq")
    planes = size // PLANE
    rows, width = features.shape
    own_cols = width // size
    group = own_cols * planes
    block = ((rows, width), BF16)
    wide = ((rows, width), F32)
    far_up = far_pieces(upstream)
    acts = gelu_pair(features)[0].astype(BF16)
    edge = moved(acts, lambda i: {0: i - 2, 3: i + 2}.get((i // 2) % 4))
    flip, turn, cross = (moved(acts, lambda i, s=s: i ^ (2 * s)) for s in (1, 3, 2))

    conv, back, slope = call(
        center_body, "center", [wide, wide, wide],
        features, acts, upstream, first_taps, second_taps,
    )
    flip, turn, cross, edge, conv, back, *far_up = lax.optimization_barrier(
        (flip, turn, cross, edge, conv, back, *far_up)
    )
    line, line_first, line_last = call(
        line_body, "line", [((4 * rows, width), BF16), block, block],
        acts, flip, turn, cross,
    )
    other_line = moved(line, lambda i: i ^ 1)
    halo_back = moved(line_last, lambda i: i + PLANE)
    halo_ahead = moved(line_first, lambda i: i - PLANE)

    part = ((2, group, rows), BF16)
    output_first, acts_second, middle, *parts = call(
        functools.partial(middle_body, planes=planes), "middle",
        [block, block, block, part, part, part, part],
        *far_up, line, edge, conv, upstream, back, first_taps, second_taps,
        scratch=[pltpu.VMEM((PLANE, group, rows), F32), pltpu.VMEM((2, rows, width), BF16)],
    )
    parts = [parts[0]] + [moved(parts[s], lambda i, s=s: i ^ (2 * s)) for s in (1, 2, 3)]
    gathered = jnp.stack([p[1] for p in parts])
    other_parts = moved(gathered, lambda i: i ^ 1)

    other_back, other_ahead = (moved(h, lambda i: i ^ 1) for h in (halo_back, halo_ahead))
    far_second = far_pieces(acts_second)

    piece = ((3, own_cols, width), BF16)
    outs = [((3, own_cols, width), F32), piece, piece, piece]
    if planes != 4:
        outs = [((3, planes, own_cols, width), F32)]
    terms = call(
        functools.partial(terms_body, planes=planes), "terms", outs,
        *parts, other_parts, line, other_line, halo_back, halo_ahead, other_back, other_ahead,
        scratch=[
            pltpu.VMEM((2, group, 4 * rows), BF16),
            pltpu.VMEM((2, 6 * rows, width), BF16),
            pltpu.VMEM((3, planes, own_cols, width), F32),
        ],
    )
    terms, far_second = lax.optimization_barrier((terms, far_second))
    if planes == 4:
        got = [moved(terms[s], lambda i, s=s: i ^ (PLANE * s)) for s in (1, 2, 3)]
        total = terms[0] + sum(g.astype(F32) for g in got)
    else:
        lines = [list(range(r, size, PLANE)) for r in range(PLANE)]
        total = lax.psum_scatter(terms[0], "seq", scatter_dimension=1, axis_index_groups=lines)
    first_taps_gradient = jnp.swapaxes(total, 1, 2)

    middle, acts_second = lax.optimization_barrier((middle, acts_second, terms[0]))[:2]
    behind = moved(middle, lambda i: i + 2)
    ahead = moved(middle, lambda i: i - 2)
    (second_layer_output,) = call(
        second_forward, "second_forward", [block],
        *far_second, acts_second, output_first, second_taps,
    )
    (input_gradient,) = call(
        first_backward, "first_backward", [block],
        middle, behind, ahead, slope, first_taps,
    )
    return second_layer_output, input_gradient, first_taps_gradient


def solution(mesh):
    placed = (P(("groups", "seq"), None), P(), P(), P(("groups", "seq"), None))
    return jax.shard_map(
        local,
        mesh=mesh,
        in_specs=placed,
        out_specs=(
            P(("groups", "seq"), None),
            P(("groups", "seq"), None),
            P(None, "groups", "seq"),
        ),
        check_vma=False,
    )
```

```python
import functools

import jax
import jax.numpy as jnp
from jax import lax
from jax.experimental import pallas as pl
from jax.experimental.pallas import tpu as pltpu
from jax.sharding import PartitionSpec as P

DILATION_ONE = 256
DILATION_TWO = 2048
PLANE = 8
LIMIT = 8 * 2**20
F32 = jnp.float32
BF16 = jnp.bfloat16


def moved(array, target):
    size = lax.axis_size("seq")
    pairs = [(i, target(i)) for i in range(size)]
    pairs = [(i, t) for i, t in pairs if t is not None and 0 <= t < size]
    return lax.ppermute(array, "seq", pairs)


def flipped(array):
    return moved(array, lambda i: i ^ 2)


def stepped(array):
    return moved(array, lambda i: i + 2 if (i // 2) % 2 else i - 2)


def far_pieces(values):
    size = lax.axis_size("seq")
    steps = DILATION_TWO // values.shape[0]
    if 2 * steps == size:
        return [moved(values, lambda i: i ^ steps)]
    return [moved(values, lambda i: i + steps), moved(values, lambda i: i - steps)]


def gelu_pair(values):
    wide = values.astype(F32)
    return jax.jvp(jax.nn.gelu, (wide,), (jnp.ones_like(wide),))


def dot(a, b):
    return jnp.dot(a, b, preferred_element_type=F32)


def dot_t(a, b):
    return lax.dot_general(a, b, (((1,), (1,)), ((), ())), preferred_element_type=F32)


def call(body, name, outs, *arrays, held=(), scratch=()):
    vmem = pl.BlockSpec(memory_space=pltpu.VMEM)
    held = [pltpu.with_memory_space_constraint(a, pltpu.HBM) for a in held]
    return pl.pallas_call(
        body,
        name=name,
        out_shape=[jax.ShapeDtypeStruct(shape, kind) for shape, kind in outs],
        in_specs=[pl.BlockSpec(memory_space=pltpu.HBM)] * len(held) + [vmem] * len(arrays),
        out_specs=[vmem] * len(outs),
        scratch_shapes=list(scratch),
        compiler_params=pltpu.CompilerParams(vmem_limit_bytes=LIMIT),
    )(*held, *arrays)


def position(rows):
    index = lax.axis_index("seq")
    lower = (index < DILATION_TWO // rows).astype(jnp.int32)
    return (index >> 1) & 3, index & 1, index >> 3, lower


def load_body(features, up, taps, second_taps, acts, conv, back, *refs):
    held, second_held, values, cotangent, sems = refs
    pairs = [(features, values), (taps.at[1], held.at[1])]
    pairs += [(up, cotangent), (second_taps.at[1], second_held.at[1])]
    for k in (0, 2):
        pairs += [(taps.at[k], held.at[k]), (second_taps.at[k], second_held.at[k])]
    copies = [pltpu.make_async_copy(a, b, sems.at[n]) for n, (a, b) in enumerate(pairs)]
    for copy in copies:
        copy.start()
    copies[0].wait()
    copies[1].wait()
    conv[...] = values[...].astype(F32) + dot(acts[...], held[1])
    copies[2].wait()
    copies[3].wait()
    back[...] = dot_t(cotangent[...], second_held[1])
    for copy in copies[4:]:
        copy.wait()


def forward_body(flip, step, conv, taps, output, acts_second, slope):
    odd = position(flip.shape[0])[0] & 1
    result = conv[...] + dot(step[...], taps[2 * odd]) + dot(flip[...], taps[2 - 2 * odd])
    result = result.astype(BF16)
    output[...] = result
    activated, steep = gelu_pair(result)
    acts_second[...] = activated.astype(BF16)
    slope[...] = steep


def middle_body(*refs, planes):
    *far, slope, up, back, taps, middle, own, one, two, three, turned = refs
    chip, core, _, lower = position(up.shape[0])
    total = back[...]
    if len(far) == 2:
        total = total + dot_t(far[0][...], taps[2]) + dot_t(far[1][...], taps[0])
    else:
        total = total + dot_t(far[0][...], taps[2 - 2 * lower])
    value = (up[...].astype(F32) + slope[...] * total).astype(BF16)
    middle[...] = value
    flat = value.astype(F32).T
    cols = turned.shape[1] // planes
    for plane in range(planes):
        for owner in range(PLANE):
            start = (plane * PLANE + owner) * cols
            turned[owner, plane * cols : (plane + 1) * cols] = flat[start : start + cols]
    for slot, out in enumerate((own, one, two, three)):
        for other in range(2):
            out[other] = turned[2 * (chip ^ slot) + (core ^ other)].astype(BF16)


def line_body(acts, flip, step, cross, turn, line):
    rows = acts.shape[0]
    chip = position(rows)[0]
    for slot, piece in enumerate((acts, flip, cross)):
        line[pl.ds((chip ^ slot) * rows, rows)] = piece[...]
    inner = (chip == 1) | (chip == 2)

    @pl.when(inner)
    def _():
        line[pl.ds((chip ^ 3) * rows, rows)] = step[...]

    @pl.when(jnp.logical_not(inner))
    def _():
        line[pl.ds((chip ^ 3) * rows, rows)] = turn[...]


def regroup_body(*refs):
    parts, (other_parts, cols, first, last) = refs[:4], refs[4:]
    rows = first.shape[2]
    chip = position(rows)[0]
    for slot, part in enumerate(parts):
        for side, piece in enumerate((part[0], other_parts[slot])):
            for b in range(4):

                @pl.when(chip == (slot ^ b))
                def _():
                    cols[side, :, b * rows : (b + 1) * rows] = piece

            @pl.when(chip == slot)
            def _():
                first[side] = piece

            @pl.when(chip == (slot ^ 3))
            def _():
                last[side] = piece


def terms_body(cols, behind, ahead, line, other_line, *refs, planes):
    outs, (stacked, sums) = refs[:-2], refs[-2:]
    group, rows = behind.shape[1:]
    plane = position(rows)[2]
    own_cols = group // planes
    total = None
    for side, acts in enumerate((line, other_line)):
        stacked[:group, : 3 * rows] = cols[side, :, rows:]
        stacked[:group, 3 * rows :] = ahead[side]
        stacked[group : 2 * group] = cols[side]
        stacked[2 * group :, :rows] = behind[side]
        stacked[2 * group :, rows:] = cols[side, :, : 3 * rows]
        value = dot(stacked[...], acts[...])
        total = value if total is None else total + value
    for k in range(3):
        for z in range(planes):
            start = k * group + z * own_cols
            sums[k, z] = total[start : start + own_cols]
    if len(outs) == 1:
        outs[0][...] = sums[...]
    else:
        for k in range(3):
            outs[0][k] = sums[k, plane]
            for s in range(1, 4):
                outs[s][k] = sums[k, plane ^ s].astype(BF16)


def second_forward(*refs):
    *far, acts, output_first, taps, output = refs
    lower = position(acts.shape[0])[3]
    conv = dot(acts[...], taps[1])
    if len(far) == 2:
        conv = conv + dot(far[0][...], taps[0]) + dot(far[1][...], taps[2])
    else:
        conv = conv + dot(far[0][...], taps[2 * lower])
    output[...] = (output_first[...].astype(F32) + conv).astype(BF16)


def first_backward(middle, flip, step, features, taps, output):
    odd = position(middle.shape[0])[0] & 1
    back = dot_t(middle[...], taps[1])
    back = back + dot_t(step[...], taps[2 - 2 * odd]) + dot_t(flip[...], taps[2 * odd])
    slope = gelu_pair(features[...])[1]
    output[...] = (middle[...].astype(F32) + slope * back).astype(BF16)


def local(features, first_taps, second_taps, upstream):
    size = lax.axis_size("seq")
    planes = size // PLANE
    rows, width = features.shape
    own_cols = width // size
    group = own_cols * planes
    block, wide = ((rows, width), BF16), ((rows, width), F32)
    all_taps = ((3, width, width), BF16)
    part = ((2, group, rows), BF16)
    together = lax.optimization_barrier

    acts = gelu_pair(features)[0].astype(BF16)
    far_up = far_pieces(upstream)
    conv, back, first_taps, second_taps, features, upstream = call(
        load_body, "load", [wide, wide, all_taps, all_taps, block, block],
        acts, held=(features, upstream, first_taps, second_taps),
        scratch=[pltpu.SemaphoreType.DMA((8,))],
    )
    flip, step = flipped(acts), stepped(acts)
    cross = moved(acts, lambda i: i ^ 4)
    turn = moved(acts, lambda i: i ^ 6 if (i // 2) % 4 in (0, 3) else None)
    step, flip, conv = together((step, flip, conv))
    output_first, acts_second, slope = call(
        forward_body, "forward", [block, block, wide], flip, step, conv, first_taps
    )
    middle, *parts = call(
        functools.partial(middle_body, planes=planes), "middle",
        [block, part, part, part, part],
        *far_up, slope, upstream, back, second_taps,
        scratch=[pltpu.VMEM((PLANE, group, rows), F32)],
    )

    cross, turn, *parts = together((cross, turn, *parts))
    parts = [parts[0]] + [moved(parts[s], lambda i, s=s: i ^ (2 * s)) for s in (1, 2, 3)]
    far_second = far_pieces(acts_second)
    other_parts = moved(jnp.stack([p[1] for p in parts]), lambda i: i ^ 1)
    cols, col_first, col_last = call(
        regroup_body, "regroup", [((2, group, 4 * rows), BF16), part, part], *parts, other_parts
    )
    (line,) = call(
        line_body, "line", [((4 * rows, width), BF16)], acts, flip, step, cross, turn
    )
    other_line = moved(line, lambda i: i ^ 1)
    cols_behind = moved(col_last, lambda i: i + PLANE)
    cols_ahead = moved(col_first, lambda i: i - PLANE)
    other_line, far_second = together((other_line, far_second))

    piece = ((3, own_cols, width), BF16)
    outs = [((3, own_cols, width), F32), piece, piece, piece]
    if planes != 4:
        outs = [((3, planes, own_cols, width), F32)]
    terms = call(
        functools.partial(terms_body, planes=planes), "terms", outs,
        cols, cols_behind, cols_ahead, line, other_line,
        scratch=[
            pltpu.VMEM((3 * group, 4 * rows), BF16),
            pltpu.VMEM((3, planes, own_cols, width), F32),
        ],
    )
    late, _ = together((middle, terms[0]))
    middle_flip, middle_step = flipped(late), stepped(late)
    if planes == 4:
        got = [moved(terms[s], lambda i, s=s: i ^ (PLANE * s)) for s in (1, 2, 3)]
        total = terms[0] + sum(g.astype(F32) for g in got)
    else:
        lines = [list(range(r, size, PLANE)) for r in range(PLANE)]
        total = lax.psum_scatter(terms[0], "seq", scatter_dimension=1, axis_index_groups=lines)
    first_taps_gradient = jnp.swapaxes(total, 1, 2)

    (second_layer_output,) = call(
        second_forward, "second_forward", [block],
        *far_second, acts_second, output_first, second_taps,
    )
    (input_gradient,) = call(
        first_backward, "first_backward", [block],
        middle, middle_flip, middle_step, features, first_taps,
    )
    return second_layer_output, input_gradient, first_taps_gradient


def solution(mesh):
    placed = (P(("groups", "seq"), None), P(), P(), P(("groups", "seq"), None))
    return jax.shard_map(
        local,
        mesh=mesh,
        in_specs=placed,
        out_specs=(
            P(("groups", "seq"), None),
            P(("groups", "seq"), None),
            P(None, "groups", "seq"),
        ),
        check_vma=False,
    )
```

```python
import functools

import jax
import jax.numpy as jnp
from jax import lax
from jax.experimental import pallas as pl
from jax.experimental.pallas import tpu as pltpu
from jax.sharding import PartitionSpec as P

DILATION_ONE = 256
DILATION_TWO = 2048
PLANE = 8
LIMIT = 8 * 2**20
F32 = jnp.float32
BF16 = jnp.bfloat16


def moved(array, target):
    size = lax.axis_size("seq")
    pairs = [(i, target(i)) for i in range(size)]
    pairs = [(i, t) for i, t in pairs if t is not None and 0 <= t < size]
    return lax.ppermute(array, "seq", pairs)


def flipped(array):
    return moved(array, lambda i: i ^ 2)


def stepped(array):
    return moved(array, lambda i: i + 2 if (i // 2) % 2 else i - 2)


def far_pieces(values):
    size = lax.axis_size("seq")
    steps = DILATION_TWO // values.shape[0]
    if 2 * steps == size:
        return [moved(values, lambda i: i ^ steps)]
    return [moved(values, lambda i: i + steps), moved(values, lambda i: i - steps)]


def gelu_pair(values):
    wide = values.astype(F32)
    return jax.jvp(jax.nn.gelu, (wide,), (jnp.ones_like(wide),))


def gelu(ref):
    return jax.nn.gelu(ref[...].astype(F32)).astype(BF16)


def dot(a, b):
    return jnp.dot(a, b, preferred_element_type=F32)


def dot_t(a, b):
    return lax.dot_general(a, b, (((1,), (1,)), ((), ())), preferred_element_type=F32)


def call(body, name, outs, *arrays, held=(), scratch=()):
    vmem = pl.BlockSpec(memory_space=pltpu.VMEM)
    held = [pltpu.with_memory_space_constraint(a, pltpu.HBM) for a in held]
    return pl.pallas_call(
        body,
        name=name,
        out_shape=[jax.ShapeDtypeStruct(shape, kind) for shape, kind in outs],
        in_specs=[pl.BlockSpec(memory_space=pltpu.HBM)] * len(held) + [vmem] * len(arrays),
        out_specs=[vmem] * len(outs),
        scratch_shapes=list(scratch),
        compiler_params=pltpu.CompilerParams(vmem_limit_bytes=LIMIT),
    )(*held, *arrays)


def position(rows):
    index = lax.axis_index("seq")
    lower = (index < DILATION_TWO // rows).astype(jnp.int32)
    return (index >> 1) & 3, index & 1, index >> 3, lower


def load_body(features, up, taps, second_taps, acts, conv, back, *refs):
    held, second_held, values, cotangent, sems = refs
    pairs = [(features, values), (taps.at[1], held.at[1])]
    pairs += [(up, cotangent), (second_taps.at[1], second_held.at[1])]
    for k in (0, 2):
        pairs += [(taps.at[k], held.at[k]), (second_taps.at[k], second_held.at[k])]
    copies = [pltpu.make_async_copy(a, b, sems.at[n]) for n, (a, b) in enumerate(pairs)]
    for copy in copies:
        copy.start()
    copies[0].wait()
    acts[...] = gelu(values)
    copies[1].wait()
    conv[...] = values[...].astype(F32) + dot(acts[...], held[1])
    copies[2].wait()
    copies[3].wait()
    back[...] = dot_t(cotangent[...], second_held[1])
    for copy in copies[4:]:
        copy.wait()


def forward_body(flip, step, conv, taps, output, acts_second, slope, flip_acts, step_acts):
    odd = position(flip.shape[0])[0] & 1
    flip_acts[...] = gelu(flip)
    step_acts[...] = gelu(step)
    result = conv[...] + dot(step_acts[...], taps[2 * odd])
    result = result + dot(flip_acts[...], taps[2 - 2 * odd])
    result = result.astype(BF16)
    output[...] = result
    activated, steep = gelu_pair(result)
    acts_second[...] = activated.astype(BF16)
    slope[...] = steep


def middle_body(*refs, planes):
    *far, slope, up, back, taps, middle, own, one, two, three, turned = refs
    chip, core, _, lower = position(up.shape[0])
    total = back[...]
    if len(far) == 2:
        total = total + dot_t(far[0][...], taps[2]) + dot_t(far[1][...], taps[0])
    else:
        total = total + dot_t(far[0][...], taps[2 - 2 * lower])
    value = (up[...].astype(F32) + slope[...] * total).astype(BF16)
    middle[...] = value
    flat = value.astype(F32).T
    cols = turned.shape[1] // planes
    for plane in range(planes):
        for owner in range(PLANE):
            start = (plane * PLANE + owner) * cols
            turned[owner, plane * cols : (plane + 1) * cols] = flat[start : start + cols]
    for slot, out in enumerate((own, one, two, three)):
        for other in range(2):
            out[other] = turned[2 * (chip ^ slot) + (core ^ other)].astype(BF16)


def line_body(acts, flip, step, cross, turn, line):
    rows = acts.shape[0]
    chip = position(rows)[0]
    for slot, piece in enumerate((acts, flip)):
        line[pl.ds((chip ^ slot) * rows, rows)] = piece[...]
    line[pl.ds((chip ^ 2) * rows, rows)] = gelu(cross)
    inner = (chip == 1) | (chip == 2)

    @pl.when(inner)
    def _():
        line[pl.ds((chip ^ 3) * rows, rows)] = step[...]

    @pl.when(jnp.logical_not(inner))
    def _():
        line[pl.ds((chip ^ 3) * rows, rows)] = gelu(turn)


def regroup_body(*refs):
    parts, (other_parts, cols, first, last) = refs[:4], refs[4:]
    rows = first.shape[2]
    chip = position(rows)[0]
    for slot, part in enumerate(parts):
        for side, piece in enumerate((part[0], other_parts[slot])):
            for b in range(4):

                @pl.when(chip == (slot ^ b))
                def _():
                    cols[side, :, b * rows : (b + 1) * rows] = piece

            @pl.when(chip == slot)
            def _():
                first[side] = piece

            @pl.when(chip == (slot ^ 3))
            def _():
                last[side] = piece


def terms_body(cols, behind, ahead, line, other_line, *refs, planes):
    outs, (stacked, sums) = refs[:-2], refs[-2:]
    group, rows = behind.shape[1:]
    plane = position(rows)[2]
    own_cols = group // planes
    total = None
    for side, acts in enumerate((line, other_line)):
        stacked[:group, : 3 * rows] = cols[side, :, rows:]
        stacked[:group, 3 * rows :] = ahead[side]
        stacked[group : 2 * group] = cols[side]
        stacked[2 * group :, :rows] = behind[side]
        stacked[2 * group :, rows:] = cols[side, :, : 3 * rows]
        value = dot(stacked[...], acts[...])
        total = value if total is None else total + value
    for k in range(3):
        for z in range(planes):
            start = k * group + z * own_cols
            sums[k, z] = total[start : start + own_cols]
    if len(outs) == 1:
        outs[0][...] = sums[...]
    else:
        for k in range(3):
            outs[0][k] = sums[k, plane]
            for s in range(1, 4):
                outs[s][k] = sums[k, plane ^ s].astype(BF16)


def second_forward(*refs):
    *far, acts, output_first, taps, output = refs
    lower = position(acts.shape[0])[3]
    conv = dot(acts[...], taps[1])
    if len(far) == 2:
        conv = conv + dot(far[0][...], taps[0]) + dot(far[1][...], taps[2])
    else:
        conv = conv + dot(far[0][...], taps[2 * lower])
    output[...] = (output_first[...].astype(F32) + conv).astype(BF16)


def early_backward(middle, features, taps, partial, slope):
    slope[...] = gelu_pair(features[...])[1]
    partial[...] = dot_t(middle[...], taps[1])


def first_backward(middle, flip, step, partial, slope, taps, output):
    odd = position(middle.shape[0])[0] & 1
    back = partial[...] + dot_t(step[...], taps[2 - 2 * odd]) + dot_t(flip[...], taps[2 * odd])
    output[...] = (middle[...].astype(F32) + slope[...] * back).astype(BF16)


def local(features, first_taps, second_taps, upstream):
    size = lax.axis_size("seq")
    planes = size // PLANE
    rows, width = features.shape
    own_cols = width // size
    group = own_cols * planes
    block, wide = ((rows, width), BF16), ((rows, width), F32)
    all_taps = ((3, width, width), BF16)
    part = ((2, group, rows), BF16)
    together = lax.optimization_barrier

    far_up = far_pieces(upstream)
    flip, step = flipped(features), stepped(features)
    cross = moved(features, lambda i: i ^ 4)
    turn = moved(features, lambda i: i ^ 6 if (i // 2) % 4 in (0, 3) else None)
    acts, conv, back, first_taps, second_taps, features, upstream = call(
        load_body, "load", [block, wide, wide, all_taps, all_taps, block, block],
        held=(features, upstream, first_taps, second_taps),
        scratch=[pltpu.SemaphoreType.DMA((8,))],
    )
    step, flip, conv = together((step, flip, conv))
    output_first, acts_second, slope, flip, step = call(
        forward_body, "forward", [block, block, wide, block, block], flip, step, conv, first_taps
    )
    middle, *parts = call(
        functools.partial(middle_body, planes=planes), "middle",
        [block, part, part, part, part],
        *far_up, slope, upstream, back, second_taps,
        scratch=[pltpu.VMEM((PLANE, group, rows), F32)],
    )

    cross, turn, *parts = together((cross, turn, *parts))
    parts = [parts[0]] + [moved(parts[s], lambda i, s=s: i ^ (2 * s)) for s in (1, 2, 3)]
    far_second = far_pieces(acts_second)
    other_parts = moved(jnp.stack([p[1] for p in parts]), lambda i: i ^ 1)
    cols, col_first, col_last = call(
        regroup_body, "regroup", [((2, group, 4 * rows), BF16), part, part], *parts, other_parts
    )
    (line,) = call(
        line_body, "line", [((4 * rows, width), BF16)], acts, flip, step, cross, turn
    )
    other_line = moved(line, lambda i: i ^ 1)
    cols_behind = moved(col_last, lambda i: i + PLANE)
    cols_ahead = moved(col_first, lambda i: i - PLANE)
    other_line, far_second = together((other_line, far_second))

    piece = ((3, own_cols, width), BF16)
    outs = [((3, own_cols, width), F32), piece, piece, piece]
    if planes != 4:
        outs = [((3, planes, own_cols, width), F32)]
    terms = call(
        functools.partial(terms_body, planes=planes), "terms", outs,
        cols, cols_behind, cols_ahead, line, other_line,
        scratch=[
            pltpu.VMEM((3 * group, 4 * rows), BF16),
            pltpu.VMEM((3, planes, own_cols, width), F32),
        ],
    )
    late, _ = together((middle, terms[0]))
    middle_flip, middle_step = flipped(late), stepped(late)
    if planes == 4:
        got = [moved(terms[s], lambda i, s=s: i ^ (PLANE * s)) for s in (1, 2, 3)]
        total = terms[0] + sum(g.astype(F32) for g in got)
    else:
        lines = [list(range(r, size, PLANE)) for r in range(PLANE)]
        total = lax.psum_scatter(terms[0], "seq", scatter_dimension=1, axis_index_groups=lines)
    first_taps_gradient = jnp.swapaxes(total, 1, 2)

    partial, slope_first = call(
        early_backward, "early_backward", [wide, wide], late, features, first_taps
    )
    (second_layer_output,) = call(
        second_forward, "second_forward", [block],
        *far_second, acts_second, output_first, second_taps,
    )
    (input_gradient,) = call(
        first_backward, "first_backward", [block],
        middle, middle_flip, middle_step, partial, slope_first, first_taps,
    )
    return second_layer_output, input_gradient, first_taps_gradient


def solution(mesh):
    placed = (P(("groups", "seq"), None), P(), P(), P(("groups", "seq"), None))
    return jax.shard_map(
        local,
        mesh=mesh,
        in_specs=placed,
        out_specs=(
            P(("groups", "seq"), None),
            P(("groups", "seq"), None),
            P(None, "groups", "seq"),
        ),
        check_vma=False,
    )
```

```python
import functools

import jax
import jax.numpy as jnp
from jax import lax
from jax.experimental import pallas as pl
from jax.experimental.pallas import tpu as pltpu
from jax.sharding import PartitionSpec as P

DILATION_ONE = 256
DILATION_TWO = 2048
PLANE = 8
LIMIT = 8 * 2**20
F32 = jnp.float32
BF16 = jnp.bfloat16


def moved(array, target):
    size = lax.axis_size("seq")
    pairs = [(i, target(i)) for i in range(size)]
    pairs = [(i, t) for i, t in pairs if t is not None and 0 <= t < size]
    return lax.ppermute(array, "seq", pairs)


def flipped(array):
    return moved(array, lambda i: i ^ 2)


def stepped(array):
    return moved(array, lambda i: i + 2 if (i // 2) % 2 else i - 2)


def far_pieces(values):
    size = lax.axis_size("seq")
    steps = DILATION_TWO // values.shape[0]
    if 2 * steps == size:
        return [moved(values, lambda i: i ^ steps)]
    return [moved(values, lambda i: i + steps), moved(values, lambda i: i - steps)]


def gelu_pair(values):
    wide = values.astype(F32)
    return jax.jvp(jax.nn.gelu, (wide,), (jnp.ones_like(wide),))


def gelu(ref):
    return jax.nn.gelu(ref[...].astype(F32)).astype(BF16)


def dot(a, b):
    return jnp.dot(a, b, preferred_element_type=F32)


def dot_t(a, b):
    return lax.dot_general(a, b, (((1,), (1,)), ((), ())), preferred_element_type=F32)


def call(body, name, outs, *arrays, held=(), scratch=()):
    vmem = pl.BlockSpec(memory_space=pltpu.VMEM)
    held = [pltpu.with_memory_space_constraint(a, pltpu.HBM) for a in held]
    return pl.pallas_call(
        body,
        name=name,
        out_shape=[jax.ShapeDtypeStruct(shape, kind) for shape, kind in outs],
        in_specs=[pl.BlockSpec(memory_space=pltpu.HBM)] * len(held) + [vmem] * len(arrays),
        out_specs=[vmem] * len(outs),
        scratch_shapes=list(scratch),
        compiler_params=pltpu.CompilerParams(vmem_limit_bytes=LIMIT),
    )(*held, *arrays)


def position(rows):
    index = lax.axis_index("seq")
    lower = (index < DILATION_TWO // rows).astype(jnp.int32)
    return (index >> 1) & 3, index & 1, index >> 3, lower


def load_body(features, up, taps, second_taps, acts, conv, back, *refs):
    held, second_held, values, cotangent, sems = refs
    pairs = [(features, values), (taps.at[1], held.at[1])]
    pairs += [(up, cotangent), (second_taps.at[1], second_held.at[1])]
    for k in (0, 2):
        pairs += [(taps.at[k], held.at[k]), (second_taps.at[k], second_held.at[k])]
    copies = [pltpu.make_async_copy(a, b, sems.at[n]) for n, (a, b) in enumerate(pairs)]
    for copy in copies:
        copy.start()
    copies[0].wait()
    acts[...] = gelu(values)
    copies[1].wait()
    conv[...] = values[...].astype(F32) + dot(acts[...], held[1])
    copies[2].wait()
    copies[3].wait()
    back[...] = dot_t(cotangent[...], second_held[1])
    for copy in copies[4:]:
        copy.wait()


def forward_body(flip, step, conv, taps, output, acts_second, slope, flip_acts, step_acts):
    odd = position(flip.shape[0])[0] & 1
    flip_acts[...] = gelu(flip)
    step_acts[...] = gelu(step)
    result = conv[...] + dot(step_acts[...], taps[2 * odd])
    result = result + dot(flip_acts[...], taps[2 - 2 * odd])
    result = result.astype(BF16)
    output[...] = result
    activated, steep = gelu_pair(result)
    acts_second[...] = activated.astype(BF16)
    slope[...] = steep


def middle_body(*refs, planes):
    *far, slope, up, back, taps, middle, own, one, two, three, turned = refs
    chip, core, _, lower = position(up.shape[0])
    total = back[...]
    if len(far) == 2:
        total = total + dot_t(far[0][...], taps[2]) + dot_t(far[1][...], taps[0])
    else:
        total = total + dot_t(far[0][...], taps[2 - 2 * lower])
    value = (up[...].astype(F32) + slope[...] * total).astype(BF16)
    middle[...] = value
    flat = value.astype(F32).T
    cols = turned.shape[1] // planes
    for plane in range(planes):
        for owner in range(PLANE):
            start = (plane * PLANE + owner) * cols
            turned[owner, plane * cols : (plane + 1) * cols] = flat[start : start + cols]
    for slot, out in enumerate((own, one, two, three)):
        for other in range(2):
            out[other] = turned[2 * (chip ^ slot) + (core ^ other)].astype(BF16)


def line_body(acts, flip, step, cross, turn, line):
    rows = acts.shape[0]
    chip = position(rows)[0]
    for slot, piece in enumerate((acts, flip)):
        line[pl.ds((chip ^ slot) * rows, rows)] = piece[...]
    line[pl.ds((chip ^ 2) * rows, rows)] = gelu(cross)
    inner = (chip == 1) | (chip == 2)

    @pl.when(inner)
    def _():
        line[pl.ds((chip ^ 3) * rows, rows)] = step[...]

    @pl.when(jnp.logical_not(inner))
    def _():
        line[pl.ds((chip ^ 3) * rows, rows)] = gelu(turn)


def regroup_body(*refs):
    parts, (other_parts, cols, first, last) = refs[:4], refs[4:]
    rows = first.shape[2]
    chip = position(rows)[0]
    for slot, part in enumerate(parts):
        for side, piece in enumerate((part[0], other_parts[slot])):
            for b in range(4):

                @pl.when(chip == (slot ^ b))
                def _():
                    cols[side, :, b * rows : (b + 1) * rows] = piece

            @pl.when(chip == slot)
            def _():
                first[side] = piece

            @pl.when(chip == (slot ^ 3))
            def _():
                last[side] = piece


def terms_body(cols, behind, ahead, line, other_line, *refs, planes):
    outs, (stacked, sums) = refs[:-2], refs[-2:]
    group, rows = behind.shape[1:]
    plane = position(rows)[2]
    own_cols = group // planes
    total = None
    for side, acts in enumerate((line, other_line)):
        stacked[:group, : 3 * rows] = cols[side, :, rows:]
        stacked[:group, 3 * rows :] = ahead[side]
        stacked[group : 2 * group] = cols[side]
        stacked[2 * group :, :rows] = behind[side]
        stacked[2 * group :, rows:] = cols[side, :, : 3 * rows]
        value = dot(stacked[...], acts[...])
        total = value if total is None else total + value
    for k in range(3):
        for z in range(planes):
            start = k * group + z * own_cols
            sums[k, z] = total[start : start + own_cols]
    if len(outs) == 1:
        outs[0][...] = sums[...]
    else:
        for k in range(3):
            outs[0][k] = sums[k, plane]
            for s in range(1, 4):
                outs[s][k] = sums[k, plane ^ s].astype(BF16)


def second_forward(*refs):
    *far, acts, output_first, taps, output = refs
    lower = position(acts.shape[0])[3]
    conv = dot(acts[...], taps[1])
    if len(far) == 2:
        conv = conv + dot(far[0][...], taps[0]) + dot(far[1][...], taps[2])
    else:
        conv = conv + dot(far[0][...], taps[2 * lower])
    output[...] = (output_first[...].astype(F32) + conv).astype(BF16)


def early_backward(middle, features, taps, partial, slope, step_tap, flip_tap):
    odd = position(middle.shape[0])[0] & 1
    step_tap[...] = taps[2 - 2 * odd].T
    flip_tap[...] = taps[2 * odd].T
    slope[...] = gelu_pair(features[...])[1]
    partial[...] = dot_t(middle[...], taps[1])


def first_backward(middle, flip, step, partial, slope, step_tap, flip_tap, output):
    back = partial[...] + dot(step[...], step_tap[...]) + dot(flip[...], flip_tap[...])
    output[...] = (middle[...].astype(F32) + slope[...] * back).astype(BF16)


def local(features, first_taps, second_taps, upstream):
    size = lax.axis_size("seq")
    planes = size // PLANE
    rows, width = features.shape
    own_cols = width // size
    group = own_cols * planes
    block, wide = ((rows, width), BF16), ((rows, width), F32)
    all_taps = ((3, width, width), BF16)
    part = ((2, group, rows), BF16)
    together = lax.optimization_barrier

    far_up = far_pieces(upstream)
    flip, step = flipped(features), stepped(features)
    cross = moved(features, lambda i: i ^ 4)
    turn = moved(features, lambda i: i ^ 6 if (i // 2) % 4 in (0, 3) else None)
    acts, conv, back, first_taps, second_taps, features, upstream = call(
        load_body, "load", [block, wide, wide, all_taps, all_taps, block, block],
        held=(features, upstream, first_taps, second_taps),
        scratch=[pltpu.SemaphoreType.DMA((8,))],
    )
    step, flip, conv = together((step, flip, conv))
    output_first, acts_second, slope, flip, step = call(
        forward_body, "forward", [block, block, wide, block, block], flip, step, conv, first_taps
    )
    middle, *parts = call(
        functools.partial(middle_body, planes=planes), "middle",
        [block, part, part, part, part],
        *far_up, slope, upstream, back, second_taps,
        scratch=[pltpu.VMEM((PLANE, group, rows), F32)],
    )

    cross, turn, *parts = together((cross, turn, *parts))
    parts = [parts[0]] + [moved(parts[s], lambda i, s=s: i ^ (2 * s)) for s in (1, 2, 3)]
    far_second = far_pieces(acts_second)
    other_parts = moved(jnp.stack([p[1] for p in parts]), lambda i: i ^ 1)
    cols, col_first, col_last = call(
        regroup_body, "regroup", [((2, group, 4 * rows), BF16), part, part], *parts, other_parts
    )
    (line,) = call(
        line_body, "line", [((4 * rows, width), BF16)], acts, flip, step, cross, turn
    )
    other_line = moved(line, lambda i: i ^ 1)
    cols_behind = moved(col_last, lambda i: i + PLANE)
    cols_ahead = moved(col_first, lambda i: i - PLANE)
    other_line, far_second = together((other_line, far_second))

    piece = ((3, own_cols, width), BF16)
    outs = [((3, own_cols, width), F32), piece, piece, piece]
    if planes != 4:
        outs = [((3, planes, own_cols, width), F32)]
    terms = call(
        functools.partial(terms_body, planes=planes), "terms", outs,
        cols, cols_behind, cols_ahead, line, other_line,
        scratch=[
            pltpu.VMEM((3 * group, 4 * rows), BF16),
            pltpu.VMEM((3, planes, own_cols, width), F32),
        ],
    )
    late, _ = together((middle, terms[0]))
    middle_flip = flipped(late)
    middle_step = stepped(together((middle, other_line))[0])
    if planes == 4:
        got = [moved(terms[s], lambda i, s=s: i ^ (PLANE * s)) for s in (1, 2, 3)]
        total = terms[0] + sum(g.astype(F32) for g in got)
    else:
        lines = [list(range(r, size, PLANE)) for r in range(PLANE)]
        total = lax.psum_scatter(terms[0], "seq", scatter_dimension=1, axis_index_groups=lines)
    first_taps_gradient = jnp.swapaxes(total, 1, 2)

    tap = ((width, width), BF16)
    partial, slope_first, *turned = call(
        early_backward, "early_backward", [wide, wide, tap, tap], late, features, first_taps
    )
    (second_layer_output,) = call(
        second_forward, "second_forward", [block],
        *far_second, acts_second, output_first, second_taps,
    )
    (input_gradient,) = call(
        first_backward, "first_backward", [block],
        middle, middle_flip, middle_step, partial, slope_first, *turned,
    )
    return second_layer_output, input_gradient, first_taps_gradient


def solution(mesh):
    placed = (P(("groups", "seq"), None), P(), P(), P(("groups", "seq"), None))
    return jax.shard_map(
        local,
        mesh=mesh,
        in_specs=placed,
        out_specs=(
            P(("groups", "seq"), None),
            P(("groups", "seq"), None),
            P(None, "groups", "seq"),
        ),
        check_vma=False,
    )
```

```python
import functools

import jax
import jax.numpy as jnp
from jax import lax
from jax.experimental import pallas as pl
from jax.experimental.pallas import tpu as pltpu
from jax.sharding import PartitionSpec as P

DILATION_ONE = 256
DILATION_TWO = 2048
PLANE = 8
LIMIT = 8 * 2**20
F32 = jnp.float32
BF16 = jnp.bfloat16


def moved(array, target):
    size = lax.axis_size("seq")
    pairs = [(i, target(i)) for i in range(size)]
    pairs = [(i, t) for i, t in pairs if t is not None and 0 <= t < size]
    return lax.ppermute(array, "seq", pairs)


def flipped(array):
    return moved(array, lambda i: i ^ 2)


def stepped(array):
    return moved(array, lambda i: i + 2 if (i // 2) % 2 else i - 2)


def far_pieces(values):
    size = lax.axis_size("seq")
    steps = DILATION_TWO // values.shape[0]
    if 2 * steps == size:
        return [moved(values, lambda i: i ^ steps)]
    return [moved(values, lambda i: i + steps), moved(values, lambda i: i - steps)]


def gelu_pair(values):
    wide = values.astype(F32)
    return jax.jvp(jax.nn.gelu, (wide,), (jnp.ones_like(wide),))


def gelu(ref):
    return jax.nn.gelu(ref[...].astype(F32)).astype(BF16)


def dot(a, b):
    return jnp.dot(a, b, preferred_element_type=F32)


def dot_t(a, b):
    return lax.dot_general(a, b, (((1,), (1,)), ((), ())), preferred_element_type=F32)


def call(body, name, outs, *arrays, held=(), scratch=()):
    vmem = pl.BlockSpec(memory_space=pltpu.VMEM)
    held = [pltpu.with_memory_space_constraint(a, pltpu.HBM) for a in held]
    return pl.pallas_call(
        body,
        name=name,
        out_shape=[jax.ShapeDtypeStruct(shape, kind) for shape, kind in outs],
        in_specs=[pl.BlockSpec(memory_space=pltpu.HBM)] * len(held) + [vmem] * len(arrays),
        out_specs=[vmem] * len(outs),
        scratch_shapes=list(scratch),
        compiler_params=pltpu.CompilerParams(vmem_limit_bytes=LIMIT),
    )(*held, *arrays)


def position(rows):
    index = lax.axis_index("seq")
    lower = (index < DILATION_TWO // rows).astype(jnp.int32)
    return (index >> 1) & 3, index & 1, index >> 3, lower


def load_body(features, up, taps, second_taps, acts, conv, back, *refs):
    held, second_held, values, cotangent, sems = refs
    pairs = [(features, values), (taps.at[1], held.at[1])]
    pairs += [(up, cotangent), (second_taps.at[1], second_held.at[1])]
    for k in (0, 2):
        pairs += [(taps.at[k], held.at[k]), (second_taps.at[k], second_held.at[k])]
    copies = [pltpu.make_async_copy(a, b, sems.at[n]) for n, (a, b) in enumerate(pairs)]
    for copy in copies:
        copy.start()
    copies[0].wait()
    acts[...] = gelu(values)
    copies[1].wait()
    conv[...] = values[...].astype(F32) + dot(acts[...], held[1])
    copies[2].wait()
    copies[3].wait()
    back[...] = dot_t(cotangent[...], second_held[1])
    for copy in copies[4:]:
        copy.wait()


def forward_body(flip, step, conv, taps, output, acts_second, slope, flip_acts, step_acts):
    odd = position(flip.shape[0])[0] & 1
    flip_acts[...] = gelu(flip)
    step_acts[...] = gelu(step)
    result = conv[...] + dot(step_acts[...], taps[2 * odd])
    result = result + dot(flip_acts[...], taps[2 - 2 * odd])
    result = result.astype(BF16)
    output[...] = result
    activated, steep = gelu_pair(result)
    acts_second[...] = activated.astype(BF16)
    slope[...] = steep


def middle_body(*refs, planes):
    *far, slope, up, back, taps, middle, own, one, two, three, turned = refs
    chip, core, _, lower = position(up.shape[0])
    total = back[...]
    if len(far) == 2:
        total = total + dot_t(far[0][...], taps[2]) + dot_t(far[1][...], taps[0])
    else:
        total = total + dot_t(far[0][...], taps[2 - 2 * lower])
    value = (up[...].astype(F32) + slope[...] * total).astype(BF16)
    middle[...] = value
    flat = value.astype(F32).T
    cols = turned.shape[1] // planes
    for plane in range(planes):
        for owner in range(PLANE):
            start = (plane * PLANE + owner) * cols
            turned[owner, plane * cols : (plane + 1) * cols] = flat[start : start + cols]
    for slot, out in enumerate((own, one, two, three)):
        for other in range(2):
            out[other] = turned[2 * (chip ^ slot) + (core ^ other)].astype(BF16)


def line_body(acts, flip, step, cross, turn, line):
    rows = acts.shape[0]
    chip = position(rows)[0]
    for slot, piece in enumerate((acts, flip)):
        line[pl.ds((chip ^ slot) * rows, rows)] = piece[...]
    line[pl.ds((chip ^ 2) * rows, rows)] = gelu(cross)
    inner = (chip == 1) | (chip == 2)

    @pl.when(inner)
    def _():
        line[pl.ds((chip ^ 3) * rows, rows)] = step[...]

    @pl.when(jnp.logical_not(inner))
    def _():
        line[pl.ds((chip ^ 3) * rows, rows)] = gelu(turn)


def regroup_body(*refs):
    parts, (other_parts, cols, first, last) = refs[:4], refs[4:]
    rows = first.shape[2]
    chip = position(rows)[0]
    for slot, part in enumerate(parts):
        for side, piece in enumerate((part[0], other_parts[slot])):
            for b in range(4):

                @pl.when(chip == (slot ^ b))
                def _():
                    cols[side, :, b * rows : (b + 1) * rows] = piece

            @pl.when(chip == slot)
            def _():
                first[side] = piece

            @pl.when(chip == (slot ^ 3))
            def _():
                last[side] = piece


def terms_body(cols, ahead, behind, line, other_line, *refs, planes):
    outs, (stacked, sums) = refs[:-2], refs[-2:]
    group, rows = behind.shape[1:]
    plane = position(rows)[2]
    own_cols = group // planes
    total = None
    for side, acts in enumerate((line, other_line)):
        stacked[:group, : 3 * rows] = cols[side, :, rows:]
        stacked[:group, 3 * rows :] = ahead[side]
        stacked[group : 2 * group] = cols[side]
        stacked[2 * group :, :rows] = behind[side]
        stacked[2 * group :, rows:] = cols[side, :, : 3 * rows]
        value = dot(stacked[...], acts[...])
        total = value if total is None else total + value
    for k in range(3):
        for z in range(planes):
            start = k * group + z * own_cols
            sums[k, z] = total[start : start + own_cols]
    if len(outs) == 1:
        outs[0][...] = sums[...]
    else:
        for k in range(3):
            outs[0][k] = sums[k, plane]
            for s in range(1, 4):
                outs[s][k] = sums[k, plane ^ s].astype(BF16)


def second_forward(*refs):
    *far, acts, output_first, taps, output = refs
    lower = position(acts.shape[0])[3]
    conv = dot(acts[...], taps[1])
    if len(far) == 2:
        conv = conv + dot(far[0][...], taps[0]) + dot(far[1][...], taps[2])
    else:
        conv = conv + dot(far[0][...], taps[2 * lower])
    output[...] = (output_first[...].astype(F32) + conv).astype(BF16)


def early_backward(middle, features, taps, partial, slope, step_tap, flip_tap):
    odd = position(middle.shape[0])[0] & 1
    step_tap[...] = taps[2 - 2 * odd].T
    flip_tap[...] = taps[2 * odd].T
    slope[...] = gelu_pair(features[...])[1]
    partial[...] = dot_t(middle[...], taps[1])


def first_backward(middle, flip, step, partial, slope, step_tap, flip_tap, output):
    back = partial[...] + dot(step[...], step_tap[...]) + dot(flip[...], flip_tap[...])
    output[...] = (middle[...].astype(F32) + slope[...] * back).astype(BF16)


def local(features, first_taps, second_taps, upstream):
    size = lax.axis_size("seq")
    planes = size // PLANE
    rows, width = features.shape
    own_cols = width // size
    group = own_cols * planes
    block, wide = ((rows, width), BF16), ((rows, width), F32)
    all_taps = ((3, width, width), BF16)
    part = ((2, group, rows), BF16)
    together = lax.optimization_barrier

    far_up = far_pieces(upstream)
    flip, step = flipped(features), stepped(features)
    cross = moved(features, lambda i: i ^ 4)
    turn = moved(features, lambda i: i ^ 6 if (i // 2) % 4 in (0, 3) else None)
    acts, conv, back, first_taps, second_taps, features, upstream = call(
        load_body, "load", [block, wide, wide, all_taps, all_taps, block, block],
        held=(features, upstream, first_taps, second_taps),
        scratch=[pltpu.SemaphoreType.DMA((8,))],
    )
    step, flip, conv = together((step, flip, conv))
    output_first, acts_second, slope, flip, step = call(
        forward_body, "forward", [block, block, wide, block, block], flip, step, conv, first_taps
    )
    middle, *parts = call(
        functools.partial(middle_body, planes=planes), "middle",
        [block, part, part, part, part],
        *far_up, slope, upstream, back, second_taps,
        scratch=[pltpu.VMEM((PLANE, group, rows), F32)],
    )

    cross, turn, parts[3] = together((cross, turn, parts[3]))
    parts = [parts[0]] + [moved(parts[s], lambda i, s=s: i ^ (2 * s)) for s in (1, 2, 3)]
    far_second = far_pieces(acts_second)
    other_parts = moved(jnp.stack([p[1] for p in parts]), lambda i: i ^ 1)
    cols, col_first, col_last = call(
        regroup_body, "regroup", [((2, group, 4 * rows), BF16), part, part], *parts, other_parts
    )
    (line,) = call(
        line_body, "line", [((4 * rows, width), BF16)], acts, flip, step, cross, turn
    )
    other_line = moved(line, lambda i: i ^ 1)
    cols_ahead = moved(col_first, lambda i: i - PLANE)
    cols_behind = moved(col_last, lambda i: i + PLANE)
    other_line, far_second = together((other_line, far_second))

    piece = ((3, own_cols, width), BF16)
    outs = [((3, own_cols, width), F32), piece, piece, piece]
    if planes != 4:
        outs = [((3, planes, own_cols, width), F32)]
    terms = call(
        functools.partial(terms_body, planes=planes), "terms", outs,
        cols, cols_ahead, cols_behind, line, other_line,
        scratch=[
            pltpu.VMEM((3 * group, 4 * rows), BF16),
            pltpu.VMEM((3, planes, own_cols, width), F32),
        ],
    )
    late, _ = together((middle, terms[0]))
    middle_flip = flipped(together((middle, other_line))[0])
    middle_step = stepped(late)
    if planes == 4:
        got = [moved(terms[s], lambda i, s=s: i ^ (PLANE * s)) for s in (1, 2, 3)]
        total = terms[0] + sum(g.astype(F32) for g in got)
    else:
        lines = [list(range(r, size, PLANE)) for r in range(PLANE)]
        total = lax.psum_scatter(terms[0], "seq", scatter_dimension=1, axis_index_groups=lines)
    first_taps_gradient = jnp.swapaxes(total, 1, 2)

    tap = ((width, width), BF16)
    partial, slope_first, *turned = call(
        early_backward, "early_backward", [wide, wide, tap, tap], late, features, first_taps
    )
    (second_layer_output,) = call(
        second_forward, "second_forward", [block],
        *far_second, acts_second, output_first, second_taps,
    )
    (input_gradient,) = call(
        first_backward, "first_backward", [block],
        middle, middle_flip, middle_step, partial, slope_first, *turned,
    )
    return second_layer_output, input_gradient, first_taps_gradient


def solution(mesh):
    placed = (P(("groups", "seq"), None), P(), P(), P(("groups", "seq"), None))
    return jax.shard_map(
        local,
        mesh=mesh,
        in_specs=placed,
        out_specs=(
            P(("groups", "seq"), None),
            P(("groups", "seq"), None),
            P(None, "groups", "seq"),
        ),
        check_vma=False,
    )
```
